1024 devices in a mesh: blk: 32 (over z), head: 32 (over x, y, core).
Axes of the slice: x: 4, y: 4, z: 32, core: 2. Of those that a mesh axis runs over, the one named last changes fastest.
Arguments:
- query: bfloat16 [16384, 8192], P(('blk', 'head')), may hold values from -6 to 6
- key: bfloat16 [16384, 1024], P(('blk', 'head')), may hold values from -6 to 6
- value: bfloat16 [16384, 1024], P(('blk', 'head')), may hold values from -6 to 6
- grad_out: bfloat16 [16384, 8192], P(('blk', 'head')), may hold values from -6 to 6
- order: int32 [32, 2], replicated, may hold values from 0 to 63, as said below
Outputs:
- attn_out: bfloat16 [16384, 8192], P('blk', 'head')
- grad_query: bfloat16 [16384, 8192], P(('blk', 'head'))
- grad_key: bfloat16 [16384, 1024], P(('blk', 'head'))
- grad_value: bfloat16 [16384, 1024], P(('blk', 'head'))
The draws below stay inside these ranges and needn't reach their ends.
Inputs may be any that keep to these rules, and one draw needn't show every extreme that they name: Row r names the two sequence segments held by block position r: some c and 63 - c, in either order; every segment appears exactly once.
All inputs are finite; a program needn't handle non-finite values.
Results may differ from the reference program's by a relative error of at most 0.03.
Values may be sent and summed in bfloat16 or wider, within the bound.
No kernel may reach another device: no remote copies, remote signals or barrier semaphores. Data moves between devices by JAX's collectives and lax.ppermute only.
A program may use at most 32 MiB of HBM per device.

```python
import math
import jax
import jax.numpy as jnp
from jax import lax

QUERY_HEADS = 64
KEY_VALUE_HEADS = 8
HEAD_SIZE = 128
CH = 256
WINDOW_BLOCKS = 3
QUERY_PER_KEY = 8
TOKEN_COUNT = 16384
N_BLK = 32


def draw_query(key, part):
    noise_seed = jax.random.fold_in(key, 11)
    sampled_values = jax.random.truncated_normal(noise_seed, -6.0, 6.0, (TOKEN_COUNT, QUERY_HEADS * HEAD_SIZE), jnp.float32)
    return sampled_values.astype(jnp.bfloat16)


def draw_key(key, part):
    noise_seed = jax.random.fold_in(key, 23)
    sampled_values = jax.random.truncated_normal(noise_seed, -6.0, 6.0, (TOKEN_COUNT, KEY_VALUE_HEADS * HEAD_SIZE), jnp.float32)
    return sampled_values.astype(jnp.bfloat16)


def draw_order(key, part):
    seeded = jax.random.fold_in(key, 37)
    key_perm, key_flip = jax.random.split(seeded)
    lower = jax.random.permutation(key_perm, N_BLK).astype(jnp.int32)
    upper = (2 * N_BLK - 1 - lower).astype(jnp.int32)
    flipped = jax.random.randint(key_flip, (N_BLK,), 0, 2)
    first = jnp.where(flipped == 1, upper, lower)
    second = jnp.where(flipped == 1, lower, upper)
    return jnp.stack([first, second], axis=1).astype(jnp.int32)


def block_levels(key, extent, pieces, least, high):
    gain = 1.0
    for dim, blocks in pieces:
        heights = jax.random.uniform(jax.random.fold_in(jax.random.fold_in(key, 6), dim), (blocks,), jnp.float32, least / len(pieces), high / len(pieces))
        gain = gain * jnp.repeat(jnp.exp(heights), extent[dim] // blocks).reshape((-1,) + (1,) * (len(extent) - 1 - dim))
    return gain


def centred(own_key, shape, width, bound, pieces=(), kind=jnp.bfloat16):
    gain = block_levels(own_key, shape, pieces, -0.22, 0.18) if pieces else 1.0
    values = jax.random.normal(own_key, shape, jnp.float32) * width * gain
    return jnp.minimum(jnp.maximum(values, -bound), bound).astype(kind)


def setup_inputs(seed: int = 0) -> dict:
    key_of = jax.random.split(jax.random.key(seed), 6)
    query = draw_query(jax.random.fold_in(key_of[5], 71), 0)
    key = draw_key(jax.random.fold_in(key_of[5], 71), 0)
    value = centred(key_of[2], (TOKEN_COUNT, KEY_VALUE_HEADS * HEAD_SIZE), 1.0, 6.0, ((0, 1024),))
    grad_out = centred(key_of[3], (TOKEN_COUNT, QUERY_HEADS * HEAD_SIZE), 1.0, 6.0, ((0, 1024),))
    order = draw_order(jax.random.fold_in(key_of[5], 71), 0)
    return {"query": query, "key": key, "value": value, "grad_out": grad_out, "order": order}


neg_big = -1e+30

def token_positions(order):
    rows = jnp.arange(TOKEN_COUNT, dtype=jnp.int32)
    block_position = rows // (2 * CH)
    slot_pos = rows // CH % 2
    return (order[block_position, slot_pos] * CH + rows % CH).astype(jnp.int32)

def round_low(values):
    lowered = lax.optimization_barrier(values.astype(jnp.bfloat16))
    return lowered.astype(jnp.float32)

def reference(query, key, value, grad_out, order):
    scale = 1.0 / math.sqrt(HEAD_SIZE)
    positions = token_positions(order)
    window_rows = 2 * CH

    def one_block(entry_index):
        block_position = entry_index // KEY_VALUE_HEADS
        key_value_group = entry_index % KEY_VALUE_HEADS
        row_start = (block_position * window_rows).astype(jnp.int32)
        col_start = (key_value_group * QUERY_PER_KEY * HEAD_SIZE).astype(jnp.int32)
        q_block = lax.dynamic_slice(query, (row_start, col_start), (window_rows, QUERY_PER_KEY * HEAD_SIZE)).reshape(window_rows, QUERY_PER_KEY, HEAD_SIZE).astype(jnp.float32)
        g_block = lax.dynamic_slice(grad_out, (row_start, col_start), (window_rows, QUERY_PER_KEY * HEAD_SIZE)).reshape(window_rows, QUERY_PER_KEY, HEAD_SIZE).astype(jnp.float32)
        key_list = []
        value_list = []
        kpos_list = []
        for lag_index in range(WINDOW_BLOCKS):
            source = ((block_position - lag_index) % N_BLK * window_rows).astype(jnp.int32)
            kv_col = (key_value_group * HEAD_SIZE).astype(jnp.int32)
            key_list.append(lax.dynamic_slice(key, (source, kv_col), (window_rows, HEAD_SIZE)))
            value_list.append(lax.dynamic_slice(value, (source, kv_col), (window_rows, HEAD_SIZE)))
            kpos_list.append(lax.dynamic_slice(positions, (source,), (window_rows,)))
        key_win = jnp.concatenate(key_list).astype(jnp.float32)
        value_win = jnp.concatenate(value_list).astype(jnp.float32)
        key_pos = jnp.concatenate(kpos_list)
        query_pos = lax.dynamic_slice(positions, (row_start,), (window_rows,))
        allowed = key_pos[None, :] <= query_pos[:, None]
        raw_scores = jnp.einsum('qhd,kd->hqk', q_block, key_win) * scale
        masked = jnp.where(allowed, raw_scores, neg_big)
        row_max = lax.optimization_barrier(jnp.max(masked, axis=2))
        row_total = lax.optimization_barrier(jnp.sum(jnp.where(allowed, jnp.exp(masked - row_max[:, :, None]), 0.0), axis=2))
        log_total = row_max + jnp.log(row_total)
        probs = jnp.where(allowed, jnp.exp(raw_scores - log_total[:, :, None]), 0.0)
        probs_low = round_low(probs)
        attn = jnp.einsum('hqk,kd->qhd', probs_low, value_win).astype(jnp.bfloat16)
        delta = lax.optimization_barrier(jnp.sum(attn.astype(jnp.float32) * g_block, axis=2)).T
        d_probs = jnp.einsum('qhd,kd->hqk', g_block, value_win)
        d_scores = round_low(probs * (d_probs - delta[:, :, None]))
        grad_q = (scale * jnp.einsum('hqk,kd->qhd', d_scores, key_win)).astype(jnp.bfloat16)
        grad_k = scale * jnp.einsum('hqk,qhd->kd', d_scores, q_block)
        grad_v = jnp.einsum('hqk,qhd->kd', probs_low, g_block)
        return (attn, grad_q, grad_k.reshape(WINDOW_BLOCKS, window_rows, HEAD_SIZE), grad_v.reshape(WINDOW_BLOCKS, window_rows, HEAD_SIZE))
    entry_list = jnp.arange(N_BLK * KEY_VALUE_HEADS, dtype=jnp.int32)
    attn_all, gq_all, gk_all, gv_all = lax.map(one_block, entry_list)

    def heads_back(stacked_values):
        return stacked_values.reshape(N_BLK, KEY_VALUE_HEADS, window_rows, QUERY_PER_KEY, HEAD_SIZE).transpose(0, 2, 1, 3, 4).reshape(TOKEN_COUNT, QUERY_HEADS * HEAD_SIZE)

    def owners(stacked_values):
        reshaped_values = stacked_values.reshape(N_BLK, KEY_VALUE_HEADS, WINDOW_BLOCKS, window_rows, HEAD_SIZE)
        summed_values = jnp.zeros((N_BLK, KEY_VALUE_HEADS, window_rows, HEAD_SIZE), jnp.float32)
        for lag_index in range(WINDOW_BLOCKS):
            summed_values = summed_values + jnp.roll(reshaped_values[:, :, lag_index], -lag_index, axis=0)
        return summed_values.transpose(0, 2, 1, 3).reshape(TOKEN_COUNT, KEY_VALUE_HEADS * HEAD_SIZE).astype(jnp.bfloat16)
    return (heads_back(attn_all), heads_back(gq_all), owners(gk_all), owners(gv_all))
```

```python
import math

import jax
import jax.numpy as jnp
from jax import lax
from jax.experimental import pallas as pl
from jax.experimental.pallas import tpu as pltpu
from jax.sharding import PartitionSpec as P


KEY_VALUE_HEADS = 8
HEAD_SIZE = 128
COPIES = 4
HALF = 256
NEG_BIG = -1e30
SCALE = 1.0 / math.sqrt(HEAD_SIZE)
SCALE_LOG2 = SCALE * math.log2(math.e)

F32 = jnp.float32
BF16 = jnp.bfloat16

VMEM = pl.BlockSpec(memory_space=pltpu.VMEM)
SMEM = pl.BlockSpec(memory_space=pltpu.SMEM)


PARAMS = pltpu.CompilerParams(vmem_limit_bytes=16 * 1024 * 1024)


def head_cols(head):
    return slice(head * HEAD_SIZE, (head + 1) * HEAD_SIZE)


def exchange(blocks):
    return lax.all_to_all(blocks, "head", split_axis=0, concat_axis=0, tiled=True)


def shifted(rows, distance):
    count = lax.axis_size("blk")
    route = [((i - distance) % count, i) for i in range(count)]
    return lax.ppermute(rows, "blk", route)


def pack_first(q_hbm, g_hbm, k_hbm, v_hbm, out_ref, kv_ref, q_ref, g_ref, sems):
    moves = [
        pltpu.make_async_copy(k_hbm, kv_ref.at[:, 0:1024], sems.at[0]),
        pltpu.make_async_copy(v_hbm, kv_ref.at[:, 1024:2048], sems.at[1]),
        pltpu.make_async_copy(q_hbm, q_ref, sems.at[2]),
        pltpu.make_async_copy(g_hbm, g_ref, sems.at[3]),
    ]
    for move in moves:
        move.start()
    for part, source in enumerate((kv_ref, q_ref, g_ref)):
        if part == 0:
            moves[0].wait()
            moves[1].wait()
        else:
            moves[part + 1].wait()
        for peer in range(out_ref.shape[0]):
            if part == 0:
                group = peer // COPIES
                out_ref[peer, :, 512:640] = source[:, head_cols(group)]
                out_ref[peer, :, 640:768] = source[:, head_cols(group + KEY_VALUE_HEADS)]
            else:
                at = (part - 1) * 256
                cols = slice(2 * peer * HEAD_SIZE, 2 * (peer + 1) * HEAD_SIZE)
                out_ref[peer, :, at : at + 256] = source[:, cols]


def pack_lags(kv1_ref, kv2_ref, out_ref):
    for peer in range(out_ref.shape[0]):
        group = peer // COPIES
        for lag, kv_ref in enumerate((kv1_ref, kv2_ref)):
            at = lag * 256
            out_ref[peer, :, at : at + 128] = kv_ref[:, head_cols(group)]
            out_ref[peer, :, at + 128 : at + 256] = kv_ref[:, head_cols(group + KEY_VALUE_HEADS)]


def sum_copies(in_ref, group, cols):
    total = in_ref[group * COPIES, :, cols].astype(F32)
    for copy in range(1, COPIES):
        total = total + in_ref[group * COPIES + copy, :, cols].astype(F32)
    return total


def unpack_lags(in_ref, one_ref, two_ref):
    for group in range(KEY_VALUE_HEADS):
        for lag, out_ref in enumerate((one_ref, two_ref)):
            for part in range(2):
                at = lag * 256 + part * 128
                total = sum_copies(in_ref, group, slice(at, at + 128))
                out_ref[:, head_cols(group + part * KEY_VALUE_HEADS)] = total.astype(BF16)


def unpack_last(in_ref, one_ref, two_ref, gq_ref, gk_ref, gv_ref):
    for peer in range(in_ref.shape[0]):
        gq_ref[:, 2 * peer * HEAD_SIZE : 2 * (peer + 1) * HEAD_SIZE] = in_ref[peer, :, 0:256]
    for group in range(KEY_VALUE_HEADS):
        for part, out_ref in enumerate((gk_ref, gv_ref)):
            at = 256 + part * 128
            total = sum_copies(in_ref, group, slice(at, at + 128))
            cols = head_cols(group + part * KEY_VALUE_HEADS)
            total = total + one_ref[:, cols].astype(F32) + two_ref[:, cols].astype(F32)
            out_ref[:, head_cols(group)] = total.astype(BF16)


def dot(a, b):
    return lax.dot_general(a, b, (((1,), (0,)), ((), ())), preferred_element_type=F32)


def dot_nt(a, b):
    return lax.dot_general(a, b, (((1,), (1,)), ((), ())), preferred_element_type=F32)


def attention(order_ref, blk_ref, own_ref, lag_ref, attn_ref, dlag_ref, down_ref, score_ref):
    count = order_ref.shape[0] // 2
    blk = blk_ref[0]

    def low_of(block):
        first, second = order_ref[2 * block], order_ref[2 * block + 1]
        low_first = first < second
        return jnp.where(low_first, 0, HALF), jnp.where(low_first, first, second)

    low, chunk = low_of(blk)
    low1, chunk1 = low_of(lax.rem(blk + (count - 1), count))
    low2, chunk2 = low_of(lax.rem(blk + (count - 2), count))
    below1, below2 = chunk > chunk1, chunk > chunk2

    def at(offset):
        return pl.ds(pl.multiple_of(offset, HALF), HALF)

    lo, hi = at(low), at(HALF - low)
    lo1, hi1 = at(low1), at(HALF - low1)
    lo2, hi2 = at(low2), at(HALF - low2)
    q_dyn1, k_dyn1 = at(jnp.where(below1, low, HALF - low)), at(jnp.where(below1, low1, HALF - low1))
    q_dyn2, k_dyn2 = at(jnp.where(below2, low, HALF - low)), at(jnp.where(below2, low2, HALF - low2))

    tiles = (
        (lo, own_ref, lo, 512, "lo"),
        (hi, own_ref, hi, 512, "hi"),
        (hi, own_ref, lo, 512, "hi"),
        (hi, lag_ref, lo1, 0, "hi"),
        (hi, lag_ref, lo2, 256, "hi"),
        (q_dyn1, lag_ref, k_dyn1, 0, below1),
        (q_dyn2, lag_ref, k_dyn2, 256, below2),
    )
    diagonal = (0, 1)
    causal = lax.broadcasted_iota(jnp.int32, (HALF, HALF), 0) <= lax.broadcasted_iota(
        jnp.int32, (HALF, HALF), 1
    )

    def fold(side, new, low_value, high_value, op):
        if isinstance(side, str):
            if side == "lo":
                return op(low_value, new), high_value
            return low_value, (new if high_value is None else op(high_value, new))
        return (
            jnp.where(side, op(low_value, new), low_value),
            jnp.where(side, high_value, op(high_value, new)),
        )

    def pick(side, low_value, high_value):
        if isinstance(side, str):
            return low_value if side == "lo" else high_value
        return jnp.where(side, low_value, high_value)

    def first_or(op):
        return lambda old, new: new if old is None else op(old, new)

    add = first_or(jnp.add)
    larger = first_or(jnp.maximum)

    d_keys = [None] * len(tiles)
    d_values = [None] * len(tiles)
    keys_t, values_t = [], []
    for _, kv_ref, k_rows, col, _ in tiles:
        keys_t.append(kv_ref[k_rows, col : col + 128].T)
        values_t.append(kv_ref[k_rows, col + 128 : col + 256].T)

    for head in range(2):
        q_cols = head_cols(head)
        g_cols = slice(256 + head * HEAD_SIZE, 256 + (head + 1) * HEAD_SIZE)
        max_lo = max_hi = None
        for index, (q_rows, kv_ref, k_rows, col, side) in enumerate(tiles):
            score = dot_nt(kv_ref[k_rows, col : col + 128], own_ref[q_rows, q_cols]) * SCALE_LOG2
            if index in diagonal:
                score = jnp.where(causal, score, NEG_BIG)
            score_ref[index] = score
            max_lo, max_hi = fold(side, jnp.max(score, axis=0, keepdims=True), max_lo, max_hi, larger)
        sum_lo = sum_hi = None
        for index, (_, _, _, _, side) in enumerate(tiles):
            weights = jnp.exp2(score_ref[index] - pick(side, max_lo, max_hi))
            score_ref[index] = weights
            sum_lo, sum_hi = fold(side, jnp.sum(weights, axis=0, keepdims=True), sum_lo, sum_hi, add)
        inv_lo, inv_hi = 1.0 / sum_lo, 1.0 / sum_hi
        out_lo = out_hi = None
        for index, (_, _, _, _, side) in enumerate(tiles):
            probs = score_ref[index] * pick(side, inv_lo, inv_hi)
            score_ref[index] = probs
            part = dot(values_t[index], probs.astype(BF16))
            out_lo, out_hi = fold(side, part, out_lo, out_hi, add)
        attn_lo, attn_hi = out_lo.T.astype(BF16), out_hi.T.astype(BF16)
        attn_ref[lo, q_cols] = attn_lo
        attn_ref[hi, q_cols] = attn_hi
        delta_lo = jnp.sum(
            (attn_lo.astype(F32) * own_ref[lo, g_cols].astype(F32)).T, axis=0, keepdims=True
        )
        delta_hi = jnp.sum(
            (attn_hi.astype(F32) * own_ref[hi, g_cols].astype(F32)).T, axis=0, keepdims=True
        )
        dq_lo = dq_hi = None
        for index, (q_rows, kv_ref, k_rows, col, side) in enumerate(tiles):
            probs = score_ref[index]
            grads = own_ref[q_rows, g_cols]
            d_probs = dot_nt(kv_ref[k_rows, col + 128 : col + 256], grads)
            d_scores = (probs * (d_probs - pick(side, delta_lo, delta_hi))).astype(BF16)
            d_values[index] = add(d_values[index], dot(probs.astype(BF16), grads))
            d_keys[index] = add(d_keys[index], dot(d_scores, own_ref[q_rows, q_cols]))
            part = dot(keys_t[index], d_scores)
            dq_lo, dq_hi = fold(side, part, dq_lo, dq_hi, add)
        down_ref[lo, q_cols] = (dq_lo * SCALE).T.astype(BF16)
        down_ref[hi, q_cols] = (dq_hi * SCALE).T.astype(BF16)

    for part, scale, found in ((0, SCALE, d_keys), (1, 1.0, d_values)):
        cols = slice(256 + part * 128, 256 + (part + 1) * 128)
        down_ref[hi, cols] = (found[1] * scale).astype(BF16)
        down_ref[lo, cols] = ((found[0] + found[2]) * scale).astype(BF16)
        for lag, (below, lo_k, hi_k) in enumerate(((below1, lo1, hi1), (below2, lo2, hi2))):
            cols = slice(lag * 256 + part * 128, lag * 256 + (part + 1) * 128)
            always, extra = found[3 + lag], found[5 + lag]
            dlag_ref[lo_k, cols] = (jnp.where(below, always + extra, always) * scale).astype(BF16)
            dlag_ref[hi_k, cols] = (jnp.where(below, 0.0, extra) * scale).astype(BF16)


def per_device(query, key, value, grad_out, order):
    peers = lax.axis_size("head")
    rows = query.shape[0]
    window = peers * rows
    shape = jax.ShapeDtypeStruct

    first, kv = pl.pallas_call(
        pack_first,
        out_shape=(shape((peers, rows, 768), BF16), shape((rows, 2048), BF16)),
        in_specs=[pl.BlockSpec(memory_space=pltpu.HBM)] * 4,
        out_specs=(VMEM, VMEM),
        scratch_shapes=[
            pltpu.VMEM((rows, 8192), BF16),
            pltpu.VMEM((rows, 8192), BF16),
            pltpu.SemaphoreType.DMA((4,)),
        ],
        name="pack_first",
    )(query, grad_out, key, value)
    own = exchange(first).reshape(window, 768)
    kv1, kv2 = shifted(kv, 1), shifted(kv, 2)
    lags = pl.pallas_call(
        pack_lags,
        out_shape=shape((peers, rows, 512), BF16),
        in_specs=[VMEM] * 2,
        out_specs=VMEM,
        compiler_params=PARAMS,
        name="pack_lags",
    )(kv1, kv2)
    lag = exchange(lags).reshape(window, 512)

    blk = lax.axis_index("blk").astype(jnp.int32).reshape(1)
    attn, d_lag, d_own = pl.pallas_call(
        attention,
        out_shape=(
            shape((window, 256), BF16),
            shape((window, 512), BF16),
            shape((window, 512), BF16),
        ),
        in_specs=[SMEM, SMEM, VMEM, VMEM],
        out_specs=(VMEM, VMEM, VMEM),
        scratch_shapes=[pltpu.VMEM((7, HALF, HALF), F32)],
        compiler_params=PARAMS,
        name="attention",
    )(order.reshape(-1), blk, own, lag)

    one, two = pl.pallas_call(
        unpack_lags,
        out_shape=(shape((rows, 2048), BF16),) * 2,
        in_specs=[VMEM],
        out_specs=(VMEM, VMEM),
        compiler_params=PARAMS,
        name="unpack_lags",
    )(exchange(d_lag.reshape(peers, rows, 512)))
    one, two = shifted(one, -1), shifted(two, -2)
    grad_query, grad_key, grad_value = pl.pallas_call(
        unpack_last,
        out_shape=(
            shape((rows, 8192), BF16),
            shape((rows, 1024), BF16),
            shape((rows, 1024), BF16),
        ),
        in_specs=[VMEM] * 3,
        out_specs=(VMEM,) * 3,
        compiler_params=PARAMS,
        name="unpack_last",
    )(exchange(d_own.reshape(peers, rows, 512)), one, two)
    return attn, grad_query, grad_key, grad_value


def solution(mesh):
    tokens = P(("blk", "head"), None)
    return jax.shard_map(
        per_device,
        mesh=mesh,
        in_specs=(tokens, tokens, tokens, tokens, P()),
        out_specs=(P("blk", "head"), tokens, tokens, tokens),
        check_vma=False,
    )
```

```python
import math

import jax
import jax.numpy as jnp
from jax import lax
from jax.experimental import pallas as pl
from jax.experimental.pallas import tpu as pltpu
from jax.sharding import PartitionSpec as P


KEY_VALUE_HEADS = 8
HEAD_SIZE = 128
COPIES = 4
HALF = 256
NEG_BIG = -1e30
SCALE = 1.0 / math.sqrt(HEAD_SIZE)
SCALE_LOG2 = SCALE * math.log2(math.e)

F32 = jnp.float32
BF16 = jnp.bfloat16

VMEM = pl.BlockSpec(memory_space=pltpu.VMEM)
SMEM = pl.BlockSpec(memory_space=pltpu.SMEM)


PARAMS = pltpu.CompilerParams(vmem_limit_bytes=16 * 1024 * 1024)


def head_cols(head):
    return slice(head * HEAD_SIZE, (head + 1) * HEAD_SIZE)


def exchange(blocks):
    return lax.all_to_all(blocks, "head", split_axis=0, concat_axis=0, tiled=True)


def shifted(rows, distance):
    count = lax.axis_size("blk")
    route = [((i - distance) % count, i) for i in range(count)]
    return lax.ppermute(rows, "blk", route)


def join_rows(k_hbm, v_hbm, kv_ref, sems):
    moves = [
        pltpu.make_async_copy(k_hbm, kv_ref.at[:, 0:1024], sems.at[0]),
        pltpu.make_async_copy(v_hbm, kv_ref.at[:, 1024:2048], sems.at[1]),
    ]
    for move in moves:
        move.start()
    for move in moves:
        move.wait()


def pack_own(order_ref, blk_ref, kv_ref, q_ref, g_ref, out_ref, facts_ref):
    count = order_ref.shape[0]
    for lag in range(3):
        block = lax.rem(blk_ref[0] + (count - lag), count)
        first, second = order_ref[block, 0], order_ref[block, 1]
        facts_ref[2 * lag] = jnp.where(first < second, 0, HALF)
        facts_ref[2 * lag + 1] = jnp.minimum(first, second)
    for peer in range(out_ref.shape[0]):
        group = peer // COPIES
        cols = slice(2 * peer * HEAD_SIZE, 2 * (peer + 1) * HEAD_SIZE)
        out_ref[peer, :, 0:256] = q_ref[:, cols]
        out_ref[peer, :, 256:512] = g_ref[:, cols]
        out_ref[peer, :, 512:640] = kv_ref[:, head_cols(group)]
        out_ref[peer, :, 640:768] = kv_ref[:, head_cols(group + KEY_VALUE_HEADS)]


def pack_lags(own_ref, kv1_ref, kv2_ref, out_ref):
    for peer in range(out_ref.shape[0]):
        group = peer // COPIES
        out_ref[peer, :, 0:768] = own_ref[peer]
        for lag, kv_ref in enumerate((kv1_ref, kv2_ref), start=1):
            at = 512 + lag * 256
            out_ref[peer, :, at : at + 128] = kv_ref[:, head_cols(group)]
            out_ref[peer, :, at + 128 : at + 256] = kv_ref[:, head_cols(group + KEY_VALUE_HEADS)]


def sum_copies(in_ref, group, cols):
    total = in_ref[group * COPIES, :, cols].astype(F32)
    for copy in range(1, COPIES):
        total = total + in_ref[group * COPIES + copy, :, cols].astype(F32)
    return total


def unpack_lags(in_ref, one_ref, two_ref):
    for group in range(KEY_VALUE_HEADS):
        for lag, out_ref in enumerate((one_ref, two_ref), start=1):
            for part in range(2):
                at = 256 + lag * 256 + part * 128
                total = sum_copies(in_ref, group, slice(at, at + 128))
                out_ref[:, head_cols(group + part * KEY_VALUE_HEADS)] = total.astype(BF16)


def unpack_query(in_ref, gq_ref):
    for peer in range(in_ref.shape[0]):
        gq_ref[:, 2 * peer * HEAD_SIZE : 2 * (peer + 1) * HEAD_SIZE] = in_ref[peer, :, 0:256]


def unpack_last(in_ref, one_ref, two_ref, gk_ref, gv_ref):
    for group in range(KEY_VALUE_HEADS):
        for part, out_ref in enumerate((gk_ref, gv_ref)):
            at = 256 + part * 128
            total = sum_copies(in_ref, group, slice(at, at + 128))
            cols = head_cols(group + part * KEY_VALUE_HEADS)
            total = total + one_ref[:, cols].astype(F32) + two_ref[:, cols].astype(F32)
            out_ref[:, head_cols(group)] = total.astype(BF16)


def dot(a, b):
    return lax.dot_general(a, b, (((1,), (0,)), ((), ())), preferred_element_type=F32)


def dot_nt(a, b):
    return lax.dot_general(a, b, (((1,), (1,)), ((), ())), preferred_element_type=F32)


def attention(facts_ref, in_ref, attn_ref, out_ref, score_ref):
    low, chunk, low1, chunk1, low2, chunk2 = (facts_ref[i] for i in range(6))
    below1, below2 = chunk > chunk1, chunk > chunk2

    def at(offset):
        return pl.ds(pl.multiple_of(offset, HALF), HALF)

    lo, hi = at(low), at(HALF - low)
    lo1, hi1 = at(low1), at(HALF - low1)
    lo2, hi2 = at(low2), at(HALF - low2)
    q_dyn1, k_dyn1 = at(jnp.where(below1, low, HALF - low)), at(jnp.where(below1, low1, HALF - low1))
    q_dyn2, k_dyn2 = at(jnp.where(below2, low, HALF - low)), at(jnp.where(below2, low2, HALF - low2))

    tiles = (
        (lo, in_ref, lo, 512, "lo"),
        (hi, in_ref, hi, 512, "hi"),
        (hi, in_ref, lo, 512, "hi"),
        (hi, in_ref, lo1, 768, "hi"),
        (hi, in_ref, lo2, 1024, "hi"),
        (q_dyn1, in_ref, k_dyn1, 768, below1),
        (q_dyn2, in_ref, k_dyn2, 1024, below2),
    )
    diagonal = (0, 1)
    causal = lax.broadcasted_iota(jnp.int32, (HALF, HALF), 0) <= lax.broadcasted_iota(
        jnp.int32, (HALF, HALF), 1
    )

    def fold(side, new, low_value, high_value, op):
        if isinstance(side, str):
            if side == "lo":
                return op(low_value, new), high_value
            return low_value, (new if high_value is None else op(high_value, new))
        return (
            jnp.where(side, op(low_value, new), low_value),
            jnp.where(side, high_value, op(high_value, new)),
        )

    def pick(side, low_value, high_value):
        if isinstance(side, str):
            return low_value if side == "lo" else high_value
        return jnp.where(side, low_value, high_value)

    def first_or(op):
        return lambda old, new: new if old is None else op(old, new)

    add = first_or(jnp.add)
    larger = first_or(jnp.maximum)

    d_keys = [None] * len(tiles)
    d_values = [None] * len(tiles)
    keys_t, values_t = [], []
    for _, kv_ref, k_rows, col, _ in tiles:
        keys_t.append(kv_ref[k_rows, col : col + 128].T)
        values_t.append(kv_ref[k_rows, col + 128 : col + 256].T)

    for head in range(2):
        q_cols = head_cols(head)
        g_cols = slice(256 + head * HEAD_SIZE, 256 + (head + 1) * HEAD_SIZE)
        max_lo = max_hi = None
        for index, (q_rows, kv_ref, k_rows, col, side) in enumerate(tiles):
            score = dot_nt(kv_ref[k_rows, col : col + 128], in_ref[q_rows, q_cols]) * SCALE_LOG2
            if index in diagonal:
                score = jnp.where(causal, score, NEG_BIG)
            score_ref[index] = score
            max_lo, max_hi = fold(side, jnp.max(score, axis=0, keepdims=True), max_lo, max_hi, larger)
        sum_lo = sum_hi = None
        for index, (_, _, _, _, side) in enumerate(tiles):
            weights = jnp.exp2(score_ref[index] - pick(side, max_lo, max_hi))
            score_ref[index] = weights
            sum_lo, sum_hi = fold(side, jnp.sum(weights, axis=0, keepdims=True), sum_lo, sum_hi, add)
        inv_lo, inv_hi = 1.0 / sum_lo, 1.0 / sum_hi
        out_lo = out_hi = None
        for index, (_, _, _, _, side) in enumerate(tiles):
            probs = score_ref[index] * pick(side, inv_lo, inv_hi)
            score_ref[index] = probs
            part = dot(values_t[index], probs.astype(BF16))
            out_lo, out_hi = fold(side, part, out_lo, out_hi, add)
        attn_lo, attn_hi = out_lo.T.astype(BF16), out_hi.T.astype(BF16)
        attn_ref[lo, q_cols] = attn_lo
        attn_ref[hi, q_cols] = attn_hi
        delta_lo = jnp.sum(
            (attn_lo.astype(F32) * in_ref[lo, g_cols].astype(F32)).T, axis=0, keepdims=True
        )
        delta_hi = jnp.sum(
            (attn_hi.astype(F32) * in_ref[hi, g_cols].astype(F32)).T, axis=0, keepdims=True
        )
        dq_lo = dq_hi = None
        for index, (q_rows, kv_ref, k_rows, col, side) in enumerate(tiles):
            probs = score_ref[index]
            grads = in_ref[q_rows, g_cols]
            d_probs = dot_nt(kv_ref[k_rows, col + 128 : col + 256], grads)
            d_scores = (probs * (d_probs - pick(side, delta_lo, delta_hi))).astype(BF16)
            d_values[index] = add(d_values[index], dot(probs.astype(BF16), grads))
            d_keys[index] = add(d_keys[index], dot(d_scores, in_ref[q_rows, q_cols]))
            part = dot(keys_t[index], d_scores)
            dq_lo, dq_hi = fold(side, part, dq_lo, dq_hi, add)
        out_ref[lo, q_cols] = (dq_lo * SCALE).T.astype(BF16)
        out_ref[hi, q_cols] = (dq_hi * SCALE).T.astype(BF16)

    for part, scale, found in ((0, SCALE, d_keys), (1, 1.0, d_values)):
        cols = slice(256 + part * 128, 256 + (part + 1) * 128)
        out_ref[hi, cols] = (found[1] * scale).astype(BF16)
        out_ref[lo, cols] = ((found[0] + found[2]) * scale).astype(BF16)
        for lag, (below, lo_k, hi_k) in enumerate(((below1, lo1, hi1), (below2, lo2, hi2))):
            at_lag = 512 + lag * 256 + part * 128
            cols = slice(at_lag, at_lag + 128)
            always, extra = found[3 + lag], found[5 + lag]
            out_ref[lo_k, cols] = (jnp.where(below, always + extra, always) * scale).astype(BF16)
            out_ref[hi_k, cols] = (jnp.where(below, 0.0, extra) * scale).astype(BF16)


def per_device(query, key, value, grad_out, order):
    peers = lax.axis_size("head")
    rows = query.shape[0]
    window = peers * rows
    shape = jax.ShapeDtypeStruct

    hbm = pl.BlockSpec(memory_space=pltpu.HBM)
    kv = pl.pallas_call(
        join_rows,
        out_shape=shape((rows, 2048), BF16),
        in_specs=[hbm] * 2,
        out_specs=VMEM,
        scratch_shapes=[pltpu.SemaphoreType.DMA((2,))],
        name="join_rows",
    )(key, value)
    kv2, kv1 = shifted(kv, 2), shifted(kv, 1)
    blk = lax.axis_index("blk").astype(jnp.int32).reshape(1)
    own, facts = pl.pallas_call(
        pack_own,
        out_shape=(shape((peers, rows, 768), BF16), shape((8,), jnp.int32)),
        in_specs=[SMEM, SMEM, VMEM, VMEM, VMEM],
        out_specs=(VMEM, SMEM),
        compiler_params=PARAMS,
        name="pack_own",
    )(order, blk, kv, query, grad_out)
    packed = pl.pallas_call(
        pack_lags,
        out_shape=shape((peers, rows, 1280), BF16),
        in_specs=[VMEM] * 3,
        out_specs=VMEM,
        compiler_params=PARAMS,
        name="pack_lags",
    )(own, kv1, kv2)
    arrived = exchange(packed).reshape(window, 1280)

    attn, grads = pl.pallas_call(
        attention,
        out_shape=(shape((window, 256), BF16), shape((window, 1024), BF16)),
        in_specs=[SMEM, VMEM],
        out_specs=(VMEM, VMEM),
        scratch_shapes=[pltpu.VMEM((7, HALF, HALF), F32)],
        compiler_params=PARAMS,
        name="attention",
    )(facts, arrived)

    back = exchange(grads.reshape(peers, rows, 1024))
    one, two = pl.pallas_call(
        unpack_lags,
        out_shape=(shape((rows, 2048), BF16),) * 2,
        in_specs=[VMEM],
        out_specs=(VMEM, VMEM),
        compiler_params=PARAMS,
        name="unpack_lags",
    )(back)
    two, one = shifted(two, -2), shifted(one, -1)
    grad_query = pl.pallas_call(
        unpack_query,
        out_shape=shape((rows, 8192), BF16),
        in_specs=[VMEM],
        out_specs=VMEM,
        compiler_params=PARAMS,
        name="unpack_query",
    )(back)
    grad_key, grad_value = pl.pallas_call(
        unpack_last,
        out_shape=(shape((rows, 1024), BF16),) * 2,
        in_specs=[VMEM] * 3,
        out_specs=(VMEM,) * 2,
        compiler_params=PARAMS,
        name="unpack_last",
    )(back, one, two)
    return attn, grad_query, grad_key, grad_value


def solution(mesh):
    tokens = P(("blk", "head"), None)
    return jax.shard_map(
        per_device,
        mesh=mesh,
        in_specs=(tokens, tokens, tokens, tokens, P()),
        out_specs=(P("blk", "head"), tokens, tokens, tokens),
        check_vma=False,
    )
```
